512 devices in a mesh: rep: 16 (over x, z_lo), mp: 32 (over z_hi, y, core).
Axes of the slice: x: 4, y: 4, z: 16 (z_hi: 4, z_lo: 4; z = z_hi * 4 + z_lo), core: 2. Of those that a mesh axis runs over, the one named last changes fastest.
Arguments:
- dense_feats: bfloat16 [65536, 13], P(('rep', 'mp')), may hold values from -6 to 6
- bag_counts: int32 [65536, 32, 64], P('rep', 'mp'), may hold values from 0 to 2
- emb_rows: bfloat16 [32, 64, 256], P('mp'), may hold values from -0.625 to 0.625
- v_emb: bfloat16 [8192, 256], P('mp'), may hold values from -0.0625 to 0.0625
- u_emb: bfloat16 [256, 8192], P(None, 'mp'), may hold values from -0.375 to 0.375
- b_emb: bfloat16 [8192], P('mp'), may hold values from -3 to 3
- v_bot: bfloat16 [256, 256], replicated, may hold values from -0.375 to 0.375
- u_bot: bfloat16 [256, 256], replicated, may hold values from -0.375 to 0.375
- b_bot: bfloat16 [256], replicated, may hold values from -3 to 3
- w_first: bfloat16 [13, 1024], replicated, may hold values from -1.75 to 1.75
- b_first: bfloat16 [1024], replicated, may hold values from -3 to 3
- w_second: bfloat16 [1024, 256], replicated, may hold values from -0.1875 to 0.1875
- b_second: bfloat16 [256], replicated, may hold values from -3 to 3
- cot_cross: bfloat16 [65536, 8192], P(('rep', 'mp')), may hold values from -24 to 24
- cot_bottom: bfloat16 [65536, 256], P(('rep', 'mp')), may hold values from -6 to 6
Outputs:
- cross_emb: bfloat16 [65536, 8192], P(('rep', 'mp'))
- cross_bot: bfloat16 [65536, 256], P(('rep', 'mp'))
- grad_table: bfloat16 [32, 64, 256], P('mp')
- grad_v_emb: bfloat16 [8192, 256], P('mp')
- grad_u_emb: bfloat16 [256, 8192], P(None, 'mp')
- grad_b_emb: bfloat16 [8192], P('mp')
- grad_v_bot: bfloat16 [256, 256], replicated
- grad_u_bot: bfloat16 [256, 256], replicated
- grad_b_bot: bfloat16 [256], replicated
- grad_w_first: bfloat16 [13, 1024], replicated
- grad_b_first: bfloat16 [1024], replicated
- grad_w_second: bfloat16 [1024, 256], replicated
- grad_b_second: bfloat16 [256], replicated
The draws below stay inside these ranges and needn't reach their ends.
Inputs may be any that keep to these rules, and one draw needn't show every extreme that they name: bag_counts[s, t, j] is how often row j of table t occurs in the bag of sample s.
All inputs are finite; a program needn't handle non-finite values.
Results may differ from the reference program's by a relative error of at most 0.029.
Values may be sent and summed in bfloat16 or wider, within the bound.
A program may use at most 64 MiB of HBM per device.

```python
import math
import jax
import jax.numpy as jnp
from jax import lax

E = 256
R = 256
H = 1024
NUM_DENSE = 13
ROWS = 64
B_DEV = 128
TABLES = 32
F = 8192
SAMPLES = 65536
N_REP = 16
N_MP = 32


def touch_ends(values, own_key, least, high):
    extent = values.shape
    spot = [jax.random.randint(jax.random.fold_in(own_key, axis), (), 0, extent[axis]) for axis in range(len(extent))]
    values = values.at[tuple(spot)].set(least)
    longest = extent.index(max(extent))
    spot[longest] = (spot[longest] + 1) % extent[longest]
    return values.at[tuple(spot)].set(high)


def strengthened(drawn, own_key, source, target, shards_of, factor):
    owner, partner = [(jnp.arange(drawn.shape[axis_at]) // (drawn.shape[axis_at] // shards_of)).reshape([-1 if axis == axis_at else 1 for axis in range(drawn.ndim)]) for axis_at in (source, target)]
    chosen = jax.random.permutation(own_key, shards_of)[partner]
    strong = (owner == chosen) | (owner == (partner + shards_of // 2) % shards_of)
    return jnp.where(strong, factor * drawn, drawn)


def shard_levels(stream_key, dims, cuts, low, top_value):
    level, own = 1.0, jax.random.fold_in(stream_key, 6)
    for position, shards_of in cuts:
        draws = jnp.exp(jax.random.uniform(jax.random.fold_in(own, position), (shards_of,), jnp.float32, low / len(cuts), top_value / len(cuts)))
        level = level * jnp.repeat(draws, dims[position] // shards_of).reshape([-1 if axis == position else 1 for axis in range(len(dims))])
    return level


def scatter_about(stream_key, shape, deviation, reach, cuts=(), held_as=jnp.bfloat16):
    values = deviation * jax.random.normal(stream_key, shape, jnp.float32)
    if cuts:
        values = values * shard_levels(stream_key, shape, cuts, -0.22, 0.18)
    return jnp.clip(values, -reach, reach).astype(held_as)


def gaussian_with(rng, extent, scale, bound, cuts, heavy, held_as=jnp.bfloat16):
    entries = scale * jax.random.normal(rng, extent, jnp.float32)
    if cuts:
        entries = entries * shard_levels(rng, extent, cuts, -0.22, 0.18)
    return jnp.clip(strengthened(entries, jax.random.fold_in(rng, 3), *heavy), -bound, bound).astype(held_as)


def setup_inputs(seed: int = 0) -> dict:
    streams_of = jax.random.split(jax.random.key(seed), 16)
    return {
        "dense_feats": scatter_about(streams_of[0], (SAMPLES, NUM_DENSE), 1.0, 6.0, ((0, 512),)),
        "bag_counts": touch_ends(jax.random.randint(streams_of[1], (SAMPLES, TABLES, ROWS), 0, 3), jax.random.fold_in(streams_of[1], 1), 0, 2).astype(jnp.int32),
        "emb_rows": scatter_about(streams_of[2], (TABLES, ROWS, E), 0.1, 0.625, ((0, 32),)),
        "v_emb": scatter_about(streams_of[3], (F, R), F ** -0.5, 0.0625, ((0, 32),)),
        "u_emb": scatter_about(streams_of[4], (R, F), R ** -0.5, 0.375, ((1, 32),)),
        "b_emb": scatter_about(streams_of[5], (F,), 0.5, 3.0, ((0, 32),)),
        "v_bot": scatter_about(streams_of[6], (E, R), E ** -0.5, 0.375),
        "u_bot": scatter_about(streams_of[7], (R, E), R ** -0.5, 0.375),
        "b_bot": scatter_about(streams_of[8], (E,), 0.5, 3.0),
        "w_first": scatter_about(streams_of[9], (NUM_DENSE, H), NUM_DENSE ** -0.5, 1.75),
        "b_first": scatter_about(streams_of[10], (H,), 0.5, 3.0),
        "w_second": scatter_about(streams_of[11], (H, E), H ** -0.5, 0.1875),
        "b_second": scatter_about(streams_of[12], (E,), 0.5, 3.0),
        "cot_cross": gaussian_with(streams_of[13], (SAMPLES, F), 1.0, 24.0, ((0, 512),), (0, 1, 512, 6.0)),
        "cot_bottom": scatter_about(streams_of[14], (SAMPLES, E), 1.0, 6.0, ((0, 512),)),
    }


def silu_slope(inputs):
    gate_value = jax.nn.sigmoid(inputs)
    return gate_value * (1.0 + inputs * (1.0 - gate_value))

def contract_rows(left_side, right_side):
    return lax.dot_general(left_side, right_side, (((0,), (0,)), ((), ())), preferred_element_type=jnp.float32)

def contract_cols(left_side, right_side):
    return lax.dot_general(left_side, right_side, (((1,), (1,)), ((), ())), preferred_element_type=jnp.float32)

def rounded(values):
    return lax.optimization_barrier(values.astype(jnp.bfloat16)).astype(jnp.float32)

def reference(dense_feats, bag_counts, emb_rows, v_emb, u_emb, b_emb, v_bot, u_bot, b_bot, w_first, b_first, w_second, b_second, cot_cross, cot_bottom):
    group_rows = B_DEV * N_MP
    grad_scale = 1.0 / math.sqrt(SAMPLES)
    first_pre = jnp.dot(dense_feats, w_first, preferred_element_type=jnp.float32) + b_first.astype(jnp.float32)
    first_act = jax.nn.silu(first_pre).astype(jnp.bfloat16)
    second_pre = jnp.dot(first_act, w_second, preferred_element_type=jnp.float32) + b_second.astype(jnp.float32)
    bottom = jax.nn.silu(second_pre).astype(jnp.bfloat16)
    emb_full = emb_rows.astype(jnp.float32)
    v_blocks = v_emb.astype(jnp.float32).reshape(TABLES, E, R)
    u_blocks = u_emb.astype(jnp.float32).reshape(R, TABLES, E)
    b_blocks = b_emb.astype(jnp.float32).reshape(TABLES, E)
    owner_mask = (jnp.arange(TABLES)[:, None] == jnp.arange(group_rows)[None, :] // B_DEV).astype(jnp.float32)
    grad_table = jnp.zeros((TABLES, ROWS, E), jnp.float32)
    grad_v = jnp.zeros((TABLES, E, R), jnp.float32)
    grad_u = jnp.zeros((R, TABLES, E), jnp.float32)
    grad_b = jnp.zeros((TABLES, E), jnp.float32)
    grad_vb = jnp.zeros((E, R), jnp.float32)
    grad_ub = jnp.zeros((R, E), jnp.float32)
    grad_bb = jnp.zeros((E,), jnp.float32)
    grad_ws = jnp.zeros((H, E), jnp.float32)
    grad_bs = jnp.zeros((E,), jnp.float32)
    grad_wf = jnp.zeros((NUM_DENSE, H), jnp.float32)
    grad_bf = jnp.zeros((H,), jnp.float32)
    cross_parts = []
    bottom_parts = []
    for replica in range(N_REP):
        lower = replica * group_rows
        upper = lower + group_rows
        counts = bag_counts[lower:upper].astype(jnp.float32)
        pooled = rounded(jnp.einsum('stj,tje->tse', counts, emb_full))
        bottom_rows = bottom[lower:upper]
        bottom_full = bottom_rows.astype(jnp.float32)
        bottom_term = jnp.dot(bottom_rows, v_bot, preferred_element_type=jnp.float32)
        low_terms = jnp.einsum('tse,ter->tsr', pooled, v_blocks) + owner_mask[:, :, None] * bottom_term[None]
        low_rank = lax.optimization_barrier(jnp.sum(rounded(low_terms), axis=0)).astype(jnp.bfloat16)
        low_full = low_rank.astype(jnp.float32)
        lift_emb = jnp.einsum('sr,rte->tse', low_full, u_blocks) + b_blocks[:, None, :]
        cross_rows = (pooled * (lift_emb + 1.0)).astype(jnp.bfloat16)
        cross_parts.append(jnp.transpose(cross_rows, (1, 0, 2)).reshape(group_rows, TABLES * E))
        lift_bottom = jnp.dot(low_rank, u_bot, preferred_element_type=jnp.float32) + b_bot.astype(jnp.float32)
        bottom_parts.append((bottom_full * (lift_bottom + 1.0)).astype(jnp.bfloat16))
        cot_rows = jnp.transpose(cot_cross[lower:upper].astype(jnp.float32).reshape(group_rows, TABLES, E), (1, 0, 2))
        d_lift = cot_rows * pooled
        d_lift_round = rounded(d_lift)
        cot_low = cot_bottom[lower:upper].astype(jnp.float32)
        d_bottom_lift = cot_low * bottom_full
        d_bottom_round = d_bottom_lift.astype(jnp.bfloat16)
        back_terms = jnp.einsum('tse,rte->tsr', d_lift_round, u_blocks)
        d_low = (lax.optimization_barrier(jnp.sum(rounded(back_terms), axis=0)) + contract_cols(d_bottom_round, u_bot)).astype(jnp.bfloat16)
        d_low_full = d_low.astype(jnp.float32)
        d_pooled = rounded(cot_rows * (lift_emb + 1.0) + jnp.einsum('sr,ter->tse', d_low_full, v_blocks))
        grad_table = grad_table + grad_scale * jnp.einsum('stj,tse->tje', counts, d_pooled)
        grad_v = grad_v + grad_scale * jnp.einsum('tse,sr->ter', pooled, d_low_full)
        grad_u = grad_u + grad_scale * jnp.einsum('sr,tse->rte', low_full, d_lift_round)
        grad_b = grad_b + grad_scale * lax.optimization_barrier(jnp.sum(d_lift, axis=1))
        d_bottom = cot_low * (lift_bottom + 1.0) + contract_cols(d_low, v_bot)
        grad_vb = grad_vb + grad_scale * contract_rows(bottom_rows, d_low)
        grad_ub = grad_ub + grad_scale * contract_rows(low_rank, d_bottom_round)
        grad_bb = grad_bb + grad_scale * lax.optimization_barrier(jnp.sum(d_bottom_lift, axis=0))
        d_second = d_bottom * silu_slope(second_pre[lower:upper])
        d_second_round = d_second.astype(jnp.bfloat16)
        grad_ws = grad_ws + grad_scale * contract_rows(first_act[lower:upper], d_second_round)
        grad_bs = grad_bs + grad_scale * lax.optimization_barrier(jnp.sum(d_second, axis=0))
        d_first = contract_cols(d_second_round, w_second) * silu_slope(first_pre[lower:upper])
        d_first_round = d_first.astype(jnp.bfloat16)
        grad_wf = grad_wf + grad_scale * contract_rows(dense_feats[lower:upper], d_first_round)
        grad_bf = grad_bf + grad_scale * lax.optimization_barrier(jnp.sum(d_first, axis=0))
    cross_emb = jnp.concatenate(cross_parts, axis=0)
    cross_bot = jnp.concatenate(bottom_parts, axis=0)
    return (cross_emb, cross_bot, grad_table.astype(jnp.bfloat16), grad_v.reshape(TABLES * E, R).astype(jnp.bfloat16), grad_u.reshape(R, TABLES * E).astype(jnp.bfloat16), grad_b.reshape(TABLES * E).astype(jnp.bfloat16), grad_vb.astype(jnp.bfloat16), grad_ub.astype(jnp.bfloat16), grad_bb.astype(jnp.bfloat16), grad_wf.astype(jnp.bfloat16), grad_bf.astype(jnp.bfloat16), grad_ws.astype(jnp.bfloat16), grad_bs.astype(jnp.bfloat16))
```

```python
import math

import jax
import jax.numpy as jnp
from jax import lax
from jax.sharding import PartitionSpec as P


def silu_slope(inputs):
    gate_value = jax.nn.sigmoid(inputs)
    return gate_value * (1.0 + inputs * (1.0 - gate_value))


def contract_rows(left_side, right_side):
    return lax.dot_general(
        left_side, right_side, (((0,), (0,)), ((), ())), preferred_element_type=jnp.float32
    )


def contract_cols(left_side, right_side):
    return lax.dot_general(
        left_side, right_side, (((1,), (1,)), ((), ())), preferred_element_type=jnp.float32
    )


def local(
    dense_feats,
    bag_counts,
    emb_rows,
    v_emb,
    u_emb,
    b_emb,
    v_bot,
    u_bot,
    b_bot,
    w_first,
    b_first,
    w_second,
    b_second,
    cot_cross,
    cot_bottom,
):
    tables = lax.axis_size("mp")
    replicas = lax.axis_size("rep")
    own_rows = dense_feats.shape[0]
    table_rows, width = emb_rows.shape[1:]
    rank = v_emb.shape[1]
    share = width // replicas
    grad_scale = 1.0 / math.sqrt(own_rows * tables * replicas)

    first = lax.axis_index("rep") * share
    pad = -(table_rows + 1) % 128
    packed = jnp.concatenate(
        [
            v_emb,
            u_emb.T,
            emb_rows[0].T,
            b_emb[:, None],
            jnp.zeros((width, pad), jnp.bfloat16),
        ],
        axis=1,
    )
    packed = lax.dynamic_slice_in_dim(packed, first, share, 0)
    packed = lax.all_gather(packed, ("mp", "rep"), axis=0, tiled=True)

    counts = bag_counts[:, 0, :].astype(jnp.bfloat16)
    counts = jnp.swapaxes(counts.reshape(tables, own_rows, table_rows), 1, 2)
    counts = lax.all_to_all(counts, "mp", split_axis=0, concat_axis=0, tiled=True)

    first_pre = jnp.dot(dense_feats, w_first, preferred_element_type=jnp.float32) + b_first.astype(
        jnp.float32
    )
    first_act = jax.nn.silu(first_pre).astype(jnp.bfloat16)
    second_pre = jnp.dot(first_act, w_second, preferred_element_type=jnp.float32) + b_second.astype(
        jnp.float32
    )
    bottom = jax.nn.silu(second_pre).astype(jnp.bfloat16)

    v_all = packed[:, :rank]
    u_all = packed[:, rank : 2 * rank]
    emb_all = packed[:, 2 * rank : 2 * rank + table_rows].reshape(tables, width, table_rows)
    b_all = packed[:, 2 * rank + table_rows].reshape(1, tables * width).astype(jnp.float32)

    pooled = lax.dot_general(
        counts, emb_all, (((1,), (2,)), ((0,), (0,))), preferred_element_type=jnp.float32
    ).astype(jnp.bfloat16)
    pooled = jnp.swapaxes(pooled, 0, 1).reshape(own_rows, tables * width)
    low_rank = (
        jnp.dot(pooled, v_all, preferred_element_type=jnp.float32)
        + jnp.dot(bottom, v_bot, preferred_element_type=jnp.float32)
    ).astype(jnp.bfloat16)
    lift_emb = contract_cols(low_rank, u_all) + b_all
    pooled_full = pooled.astype(jnp.float32)
    cross_emb = (pooled_full * (lift_emb + 1.0)).astype(jnp.bfloat16)
    lift_bottom = jnp.dot(low_rank, u_bot, preferred_element_type=jnp.float32) + b_bot.astype(
        jnp.float32
    )
    bottom_full = bottom.astype(jnp.float32)
    cross_bot = (bottom_full * (lift_bottom + 1.0)).astype(jnp.bfloat16)
    cot_rows = cot_cross.astype(jnp.float32)
    d_lift = cot_rows * pooled_full
    d_lift_round = d_lift.astype(jnp.bfloat16)
    cot_low = cot_bottom.astype(jnp.float32)
    d_bottom_lift = cot_low * bottom_full
    d_bottom_round = d_bottom_lift.astype(jnp.bfloat16)
    d_low = (
        jnp.dot(d_lift_round, u_all, preferred_element_type=jnp.float32)
        + contract_cols(d_bottom_round, u_bot)
    ).astype(jnp.bfloat16)
    d_pooled = (cot_rows * (lift_emb + 1.0) + contract_cols(d_low, v_all)).astype(jnp.bfloat16)
    d_tables = jnp.swapaxes(d_pooled.reshape(own_rows, tables, width), 0, 1)
    grad_table = lax.dot_general(
        d_tables, counts, (((1,), (2,)), ((0,), (0,))), preferred_element_type=jnp.float32
    ).reshape(tables * width, table_rows)
    grad_v = contract_rows(pooled, d_low)
    grad_u = contract_rows(d_lift_round, low_rank)
    grad_b = jnp.sum(d_lift, axis=0)
    grads = jnp.concatenate(
        [
            grad_v.astype(jnp.bfloat16),
            grad_u.astype(jnp.bfloat16),
            grad_table.astype(jnp.bfloat16),
            grad_b.astype(jnp.bfloat16)[:, None],
            jnp.zeros((tables * width, pad), jnp.bfloat16),
        ],
        axis=1,
    )
    columns = grads.shape[1]
    grads = jnp.swapaxes(grads.reshape(tables, replicas, share, columns), 0, 1)
    grads = lax.psum_scatter(
        grads.reshape(replicas * tables * share, columns), "rep", scatter_dimension=0, tiled=True
    )
    grads = lax.psum_scatter(
        grads.astype(jnp.float32) * grad_scale, "mp", scatter_dimension=0, tiled=True
    )
    grads = lax.optimization_barrier(grads).astype(jnp.bfloat16)
    grads = lax.all_gather(grads, "rep", axis=0, tiled=True)

    d_bottom = cot_low * (lift_bottom + 1.0) + contract_cols(d_low, v_bot)
    grad_vb = grad_scale * contract_rows(bottom, d_low)
    grad_ub = grad_scale * contract_rows(low_rank, d_bottom_round)
    grad_bb = grad_scale * jnp.sum(d_bottom_lift, axis=0)
    d_second = d_bottom * silu_slope(second_pre)
    d_second_round = d_second.astype(jnp.bfloat16)
    grad_ws = grad_scale * contract_rows(first_act, d_second_round)
    grad_bs = grad_scale * jnp.sum(d_second, axis=0)
    d_first = contract_cols(d_second_round, w_second) * silu_slope(first_pre)
    d_first_round = d_first.astype(jnp.bfloat16)
    grad_wf = grad_scale * contract_rows(dense_feats, d_first_round)
    grad_bf = grad_scale * jnp.sum(d_first, axis=0)
    dense_sums = lax.psum(
        (grad_wf, grad_bf, grad_ws, grad_bs, grad_vb, grad_ub, grad_bb), ("rep", "mp")
    )
    return (
        cross_emb,
        cross_bot,
        grads[:, 2 * rank : 2 * rank + table_rows].T[None],
        grads[:, :rank],
        grads[:, rank : 2 * rank].T,
        grads[:, 2 * rank + table_rows],
        dense_sums[4].astype(jnp.bfloat16),
        dense_sums[5].astype(jnp.bfloat16),
        dense_sums[6].astype(jnp.bfloat16),
        dense_sums[0].astype(jnp.bfloat16),
        dense_sums[1].astype(jnp.bfloat16),
        dense_sums[2].astype(jnp.bfloat16),
        dense_sums[3].astype(jnp.bfloat16),
    )


def solution(mesh):
    return jax.shard_map(
        local,
        mesh=mesh,
        in_specs=(
            P(("rep", "mp"), None),
            P("rep", "mp", None),
            P("mp", None, None),
            P("mp", None),
            P(None, "mp"),
            P("mp"),
            P(),
            P(),
            P(),
            P(),
            P(),
            P(),
            P(),
            P(("rep", "mp"), None),
            P(("rep", "mp"), None),
        ),
        out_specs=(
            P(("rep", "mp"), None),
            P(("rep", "mp"), None),
            P("mp", None, None),
            P("mp", None),
            P(None, "mp"),
            P("mp"),
            P(),
            P(),
            P(),
            P(),
            P(),
            P(),
            P(),
        ),
        check_vma=False,
    )
```

```python
import math

import jax
import jax.numpy as jnp
from jax import lax
from jax.sharding import PartitionSpec as P


def silu_slope(inputs):
    gate_value = jax.nn.sigmoid(inputs)
    return gate_value * (1.0 + inputs * (1.0 - gate_value))


def contract_rows(left_side, right_side):
    return lax.dot_general(
        left_side, right_side, (((0,), (0,)), ((), ())), preferred_element_type=jnp.float32
    )


def contract_cols(left_side, right_side):
    return lax.dot_general(
        left_side, right_side, (((1,), (1,)), ((), ())), preferred_element_type=jnp.float32
    )


def local(
    dense_feats,
    bag_counts,
    emb_rows,
    v_emb,
    u_emb,
    b_emb,
    v_bot,
    u_bot,
    b_bot,
    w_first,
    b_first,
    w_second,
    b_second,
    cot_cross,
    cot_bottom,
):
    tables = lax.axis_size("mp")
    replicas = lax.axis_size("rep")
    own_rows = dense_feats.shape[0]
    table_rows, width = emb_rows.shape[1:]
    rank = v_emb.shape[1]
    share = width // replicas
    grad_scale = 1.0 / math.sqrt(own_rows * tables * replicas)

    first = lax.axis_index("rep") * share
    pad = -(table_rows + 1) % 128
    packed = jnp.concatenate(
        [
            v_emb,
            u_emb.T,
            emb_rows[0].T,
            b_emb[:, None],
            jnp.zeros((width, pad), jnp.bfloat16),
        ],
        axis=1,
    )
    packed = lax.dynamic_slice_in_dim(packed, first, share, 0)
    columns = packed.shape[1]
    packed = lax.all_gather(packed, "mp", axis=0, tiled=True)
    packed = lax.all_gather(packed, "rep", axis=0, tiled=True)
    packed = jnp.swapaxes(packed.reshape(replicas, tables, share, columns), 0, 1)
    packed = packed.reshape(tables * width, columns)

    counts = bag_counts[:, 0, :].astype(jnp.bfloat16)
    counts = jnp.swapaxes(counts.reshape(tables, own_rows, table_rows), 1, 2)
    counts = lax.all_to_all(counts, "mp", split_axis=0, concat_axis=0, tiled=True)

    first_pre = jnp.dot(dense_feats, w_first, preferred_element_type=jnp.float32) + b_first.astype(
        jnp.float32
    )
    first_act = jax.nn.silu(first_pre).astype(jnp.bfloat16)
    second_pre = jnp.dot(first_act, w_second, preferred_element_type=jnp.float32) + b_second.astype(
        jnp.float32
    )
    bottom = jax.nn.silu(second_pre).astype(jnp.bfloat16)

    v_all = packed[:, :rank]
    u_all = packed[:, rank : 2 * rank]
    emb_all = packed[:, 2 * rank : 2 * rank + table_rows].reshape(tables, width, table_rows)
    b_all = packed[:, 2 * rank + table_rows].reshape(1, tables * width).astype(jnp.float32)

    pooled = lax.dot_general(
        counts, emb_all, (((1,), (2,)), ((0,), (0,))), preferred_element_type=jnp.float32
    ).astype(jnp.bfloat16)
    pooled = jnp.swapaxes(pooled, 0, 1).reshape(own_rows, tables * width)
    low_rank = (
        jnp.dot(pooled, v_all, preferred_element_type=jnp.float32)
        + jnp.dot(bottom, v_bot, preferred_element_type=jnp.float32)
    ).astype(jnp.bfloat16)
    lift_emb = contract_cols(low_rank, u_all) + b_all
    pooled_full = pooled.astype(jnp.float32)
    cross_emb = (pooled_full * (lift_emb + 1.0)).astype(jnp.bfloat16)
    lift_bottom = jnp.dot(low_rank, u_bot, preferred_element_type=jnp.float32) + b_bot.astype(
        jnp.float32
    )
    bottom_full = bottom.astype(jnp.float32)
    cross_bot = (bottom_full * (lift_bottom + 1.0)).astype(jnp.bfloat16)
    cot_rows = cot_cross.astype(jnp.float32)
    d_lift = cot_rows * pooled_full
    d_lift_round = d_lift.astype(jnp.bfloat16)
    cot_low = cot_bottom.astype(jnp.float32)
    d_bottom_lift = cot_low * bottom_full
    d_bottom_round = d_bottom_lift.astype(jnp.bfloat16)
    d_low = (
        jnp.dot(d_lift_round, u_all, preferred_element_type=jnp.float32)
        + contract_cols(d_bottom_round, u_bot)
    ).astype(jnp.bfloat16)
    d_pooled = (cot_rows * (lift_emb + 1.0) + contract_cols(d_low, v_all)).astype(jnp.bfloat16)
    d_tables = jnp.swapaxes(d_pooled.reshape(own_rows, tables, width), 0, 1)
    grad_table = lax.dot_general(
        d_tables, counts, (((1,), (2,)), ((0,), (0,))), preferred_element_type=jnp.float32
    ).reshape(tables * width, table_rows)
    grad_v = contract_rows(pooled, d_low)
    grad_u = contract_rows(d_lift_round, low_rank)
    grad_b = jnp.sum(d_lift, axis=0)
    grads = jnp.concatenate(
        [
            grad_v.astype(jnp.bfloat16),
            grad_u.astype(jnp.bfloat16),
            grad_table.astype(jnp.bfloat16),
            grad_b.astype(jnp.bfloat16)[:, None],
            jnp.zeros((tables * width, pad), jnp.bfloat16),
        ],
        axis=1,
    )
    d_bottom = cot_low * (lift_bottom + 1.0) + contract_cols(d_low, v_bot)
    grad_vb = grad_scale * contract_rows(bottom, d_low)
    grad_ub = grad_scale * contract_rows(low_rank, d_bottom_round)
    grad_bb = grad_scale * jnp.sum(d_bottom_lift, axis=0)
    d_second = d_bottom * silu_slope(second_pre)
    d_second_round = d_second.astype(jnp.bfloat16)
    grad_ws = grad_scale * contract_rows(first_act, d_second_round)
    grad_bs = grad_scale * jnp.sum(d_second, axis=0)
    d_first = contract_cols(d_second_round, w_second) * silu_slope(first_pre)
    d_first_round = d_first.astype(jnp.bfloat16)
    grad_wf = grad_scale * contract_rows(dense_feats, d_first_round)
    grad_bf = grad_scale * jnp.sum(d_first, axis=0)
    grads = jnp.swapaxes(grads.reshape(tables, replicas, share, columns), 0, 1)
    grads = grads.reshape(replicas * tables * share, columns)
    dense = (grad_wf, grad_bf, grad_ws, grad_bs, grad_vb, grad_ub, grad_bb)
    grads, dense = lax.optimization_barrier((grads, dense))
    grads = lax.psum_scatter(grads, "rep", scatter_dimension=0, tiled=True)
    dense_sums = lax.psum(dense, ("rep", "mp"))
    grads, dense_sums = lax.optimization_barrier((grads, dense_sums))
    grads = lax.psum_scatter(
        grads.astype(jnp.float32) * grad_scale, "mp", scatter_dimension=0, tiled=True
    )
    grads = lax.optimization_barrier(grads).astype(jnp.bfloat16)
    grads = lax.all_gather(grads, "rep", axis=0, tiled=True)
    return (
        cross_emb,
        cross_bot,
        grads[:, 2 * rank : 2 * rank + table_rows].T[None],
        grads[:, :rank],
        grads[:, rank : 2 * rank].T,
        grads[:, 2 * rank + table_rows],
        dense_sums[4].astype(jnp.bfloat16),
        dense_sums[5].astype(jnp.bfloat16),
        dense_sums[6].astype(jnp.bfloat16),
        dense_sums[0].astype(jnp.bfloat16),
        dense_sums[1].astype(jnp.bfloat16),
        dense_sums[2].astype(jnp.bfloat16),
        dense_sums[3].astype(jnp.bfloat16),
    )


def solution(mesh):
    return jax.shard_map(
        local,
        mesh=mesh,
        in_specs=(
            P(("rep", "mp"), None),
            P("rep", "mp", None),
            P("mp", None, None),
            P("mp", None),
            P(None, "mp"),
            P("mp"),
            P(),
            P(),
            P(),
            P(),
            P(),
            P(),
            P(),
            P(("rep", "mp"), None),
            P(("rep", "mp"), None),
        ),
        out_specs=(
            P(("rep", "mp"), None),
            P(("rep", "mp"), None),
            P("mp", None, None),
            P("mp", None),
            P(None, "mp"),
            P("mp"),
            P(),
            P(),
            P(),
            P(),
            P(),
            P(),
            P(),
        ),
        check_vma=False,
    )
```
